1024 devices in a mesh: grp: 8 (over x_hi, core), row: 8 (over y), col: 16 (over x_lo, z).
Axes of the slice: x: 8 (x_hi: 4, x_lo: 2; x = x_hi * 2 + x_lo), y: 8, z: 8, core: 2. Of those that a mesh axis runs over, the one named last changes fastest.
Arguments:
- amplitudes: bfloat16 [64, 16, 256, 256], P(('grp', 'row'), 'col'), may hold values from -6 to 6
- factors: bfloat16 [16, 256, 256], P('col'), may hold values from -0.1875 to 0.1875
- cycle_weight: bfloat16 [16384, 16384], P('col', 'row'), may hold values from -0.046875 to 0.046875
- orbital_order: int32 [256], replicated, may hold values from 0 to 255, each once
Outputs:
- ladder_term: bfloat16 [64, 16, 256, 256], P(('grp', 'row'), 'col')
- cycle_term: bfloat16 [4096, 16384], P(('grp', 'row'), 'col')
The draws below stay inside these ranges and needn't reach their ends.
Inputs may be any that keep to these rules, and one draw needn't show every extreme that they name: `orbital_order`: each of 0 to 255 appears exactly once.
All inputs are finite; a program needn't handle non-finite values.
Results may differ from the reference program's by a relative error of at most 0.0049.
Values may be sent and summed in bfloat16 or wider, within the bound.
No kernel may reach another device: no remote copies, remote signals or barrier semaphores. Data moves between devices by JAX's collectives and lax.ppermute only.
A program may use at most 64 MiB of HBM per device.

```python
import jax
import jax.numpy as jnp
from jax import lax

OCC = 64
VIRT = 256
NAUX = 16
JW = 16
NPH = 16384
PANELS = 8
PANEL_V = 32
COLS = 4096


def level_of(own_key, extent, split, smallest, top_value):
    def one(position, blocks):
        steps = jax.random.uniform(jax.random.fold_in(jax.random.fold_in(own_key, 6), position), (blocks,), jnp.float32, smallest / len(split), top_value / len(split))
        return jnp.repeat(jnp.exp(steps), extent[position] // blocks).reshape((-1,) + (1,) * (len(extent) - position - 1))

    level = one(*split[0])
    for cut in split[1:]:
        level = level * one(*cut)
    return level


def bell_draw(key, shape, spread, limit, shards=(), held_as=jnp.bfloat16):
    loudness = level_of(key, shape, shards, -0.22, 0.18) if shards else 1.0
    array = jax.random.normal(key, shape, jnp.float32) * spread * loudness
    return jnp.minimum(jnp.maximum(array, -limit), limit).astype(held_as)


def setup_inputs(seed: int = 0) -> dict:
    splits = jax.random.split(jax.random.key(seed), 5)
    amplitudes = bell_draw(splits[0], (OCC, JW, VIRT, VIRT), 1.0, 6.0, ((0, 64), (1, 16)))
    factors = bell_draw(splits[1], (NAUX, VIRT, VIRT), (VIRT * 4) ** -0.5, 0.1875, ((0, 16),))
    cycle_weight = bell_draw(splits[2], (NPH, NPH), NPH ** -0.5, 0.046875, ((0, 16), (1, 8)))
    orbital_order = jax.random.permutation(splits[3], VIRT).astype(jnp.int32)
    return {"amplitudes": amplitudes, "factors": factors, "cycle_weight": cycle_weight, "orbital_order": orbital_order}


def reference(amplitudes, factors, cycle_weight, orbital_order):
    pairs_wide = amplitudes.astype(jnp.float32)

    def add_factor(running, factor):
        factor_wide = factor.astype(jnp.float32)
        dressed = jnp.einsum("ac,kjcd->kjad", factor_wide, pairs_wide, precision=lax.Precision.HIGHEST)
        dressed = lax.optimization_barrier(dressed.astype(jnp.bfloat16)).astype(jnp.float32)
        update = jnp.einsum("kjad,bd->kjab", dressed, factor_wide, precision=lax.Precision.HIGHEST)
        return running + update, None

    zero_sum = jnp.zeros((OCC, JW, VIRT, VIRT), jnp.float32)
    ladder_sum, unused = lax.scan(add_factor, zero_sum, factors)
    ordered = jnp.take(amplitudes, orbital_order, axis=3)
    ordered = ordered.reshape(OCC, JW, VIRT, PANELS, PANEL_V)
    panel = jnp.transpose(ordered, (2, 0, 3, 1, 4)).reshape(NPH, COLS)
    cycle_sum = jnp.dot(cycle_weight.astype(jnp.float32), panel.astype(jnp.float32), precision=lax.Precision.HIGHEST)
    return ladder_sum.astype(jnp.bfloat16), cycle_sum.T.astype(jnp.bfloat16)
```

```python
import jax
import jax.numpy as jnp
from jax import lax
from jax.sharding import PartitionSpec as P


def half_groups(size):
    return [list(range(0, size // 2)), list(range(size // 2, size))]


def shards(amplitudes, factors, cycle_weight, orbital_order):
    virtual = amplitudes.shape[2]
    pair = amplitudes.reshape(virtual, virtual)
    groups = lax.axis_size("grp")
    rows = lax.axis_size("row")
    cols = lax.axis_size("col")
    width = virtual // groups
    block = virtual // rows
    all_factors = lax.all_gather(factors, "col", axis=0, tiled=True)

    pick = (orbital_order[:, None] == jnp.arange(virtual, dtype=jnp.int32)[None, :]).astype(jnp.bfloat16)
    ordered = jnp.einsum("xd,cd->xc", pick, pair, preferred_element_type=jnp.float32).astype(jnp.bfloat16)
    tiles = ordered.reshape(groups, width, rows, block)
    tiles = jnp.transpose(tiles, (0, 2, 1, 3)).reshape(groups * rows, width * block // 128, 128)
    arrived = lax.all_to_all(tiles, ("grp", "row"), 0, 0, tiled=True)
    column = arrived.reshape(groups * rows, width, block)
    column = jnp.transpose(column, (1, 2, 0)).reshape(width, block * groups * rows)

    depth = cols // 2
    copies = jnp.broadcast_to(column, (depth, *column.shape))
    near = lax.all_to_all(copies, "col", 0, 0, axis_index_groups=half_groups(cols), tiled=True)
    far = lax.ppermute(near, "col", [(i, (i + depth) % cols) for i in range(cols)])
    low = lax.axis_index("col") < depth
    first = jnp.where(low, near, far)
    second = jnp.where(low, far, near)
    panel = jnp.concatenate([first, second]).reshape(cols * width, -1)

    products = lax.dot_general(
        panel, cycle_weight, (((1,), (1,)), ((), ())), preferred_element_type=jnp.float32
    ).astype(jnp.bfloat16)
    parts = products.reshape(rows, cols * width // rows, -1)
    parts = lax.all_to_all(parts, "row", 0, 0, tiled=True)
    cycle_term = jnp.sum(parts.astype(jnp.float32), axis=0).astype(jnp.bfloat16)

    dressed = jnp.einsum(
        "pac,cd->pad", all_factors, pair, preferred_element_type=jnp.float32
    ).astype(jnp.bfloat16)
    ladder = jnp.einsum("pad,pbd->ab", dressed, all_factors, preferred_element_type=jnp.float32)
    ladder_term = ladder.astype(jnp.bfloat16).reshape(amplitudes.shape)
    return (ladder_term, cycle_term)


def solution(mesh):
    return jax.shard_map(
        shards,
        mesh=mesh,
        in_specs=(P(("grp", "row"), "col", None, None), P("col", None, None), P("col", "row"), P()),
        out_specs=(P(("grp", "row"), "col", None, None), P(("grp", "row"), "col")),
        check_vma=False,
    )
```

```python
import jax
import jax.numpy as jnp
from jax import lax
from jax.experimental import pallas as pl
from jax.experimental.pallas import tpu as pltpu
from jax.sharding import Mesh, PartitionSpec as P

AXES = ("hi", "core", "rowpair", "side", "lo", "z")


SHIFTS = (3, -3, 2, -2, 1, -1, 4)


def shift(x, by):
    depth = lax.axis_size("z")
    return lax.ppermute(x, "z", [(i, (i + by) % depth) for i in range(depth)])


def swap(x, axis):
    return lax.ppermute(x, axis, [(0, 1), (1, 0)])


def tied(x, *after):
    return lax.optimization_barrier((x, *after))[0]


def exchange(x, axes):
    return lax.all_to_all(x, axes, 0, 0, tiled=True)


def in_order(mine, other, axis, dim):
    first = lax.axis_index(axis) == 0
    return jnp.concatenate([jnp.where(first, mine, other), jnp.where(first, other, mine)], axis=dim)


def join_kernel(*refs):
    pieces, out_ref = refs[:-1], refs[-1]
    count = pieces[0].shape[0]
    for i, piece in enumerate(pieces):
        out_ref[pl.ds(i * count, count)] = piece[...]


def joined(blocks):
    shape = (len(blocks) * blocks[0].shape[0], *blocks[0].shape[1:])
    size = 4 * blocks[0].size * len(blocks)
    return pl.pallas_call(
        join_kernel,
        in_specs=[pl.BlockSpec(memory_space=pltpu.VMEM)] * len(blocks),
        out_specs=pl.BlockSpec(memory_space=pltpu.VMEM),
        out_shape=jax.ShapeDtypeStruct(shape, blocks[0].dtype),
        cost_estimate=pl.CostEstimate(flops=0, bytes_accessed=size, transcendentals=0),
        name="join",
    )(*blocks)


def product(panel, weight):
    return lax.dot_general(panel, weight, (((1,), (1,)), ((), ())), preferred_element_type=jnp.float32)


def sums_of(panel, weights):
    panel = panel.reshape(-1, panel.shape[-1])
    inner = panel.shape[1] // 2
    here, there = panel[:, :inner], panel[:, inner:]
    return jnp.concatenate(
        [(product(here, a) + product(there, b)).astype(jnp.bfloat16) for a, b in weights], axis=1
    )


def body(amplitudes, factors, cycle_weight, orbital_order):
    virtual = amplitudes.shape[2]
    pair = amplitudes.reshape(virtual, virtual)
    groups = lax.axis_size("hi") * lax.axis_size("core")
    pairs = lax.axis_size("rowpair")
    depth = lax.axis_size("z")
    occupied = groups * pairs * 2
    width = virtual // groups // 2
    block = virtual // pairs
    outs, inner = cycle_weight.shape
    core = lax.axis_index("core")

    half = virtual // 2
    mine = lax.dynamic_slice_in_dim(factors, core * half, half, axis=1)
    both = jnp.concatenate([mine, swap(mine, "lo")])

    pick = (orbital_order[:, None] == jnp.arange(virtual, dtype=jnp.int32)[None, :]).astype(jnp.bfloat16)
    ordered = jnp.einsum("xd,cd->xc", pick, pair, preferred_element_type=jnp.float32).astype(jnp.bfloat16)
    tiles = ordered.reshape(groups, 2, width, pairs, block)
    tiles = jnp.transpose(tiles, (0, 3, 1, 2, 4)).reshape(occupied, width * block // 128, 128)
    arrived = exchange(tiles, ("hi", "core", "rowpair", "side"))

    part = outs // 2
    near_weight = lax.dynamic_slice_in_dim(cycle_weight, core * part, part, axis=0)
    last_weight = lax.dynamic_slice_in_dim(cycle_weight, (1 - core) * part, part, axis=0)
    near_other = swap(near_weight, "side")
    last_other = swap(near_other, "core")

    own = arrived.reshape(occupied, width, 2, block // 2)
    own = jnp.transpose(own, (2, 1, 3, 0)).reshape(2, width, inner)
    first = lax.axis_index("side") == 0
    own = jnp.concatenate([jnp.where(first, own[0], own[1]), jnp.where(first, own[1], own[0])], axis=1)

    copies = jnp.broadcast_to(own, (depth, *own.shape))
    near = exchange(copies, "z")
    blocks = [both] + [shift(both, by) for by in SHIFTS]

    far = swap(near, "lo")
    weights = ((near_weight, near_other), (last_weight, last_other))
    near_sums = sums_of(near, weights)
    far_sums = sums_of(tied(far, near_sums), weights)
    parts = in_order(near_sums.reshape(pairs, -1, outs), far_sums.reshape(pairs, -1, outs), "lo", 0)
    parts = exchange(parts, ("rowpair", "side"))
    halves = joined(blocks)
    others = swap(halves, "core")
    whole = jnp.concatenate([halves, others], axis=1)
    dressed = jnp.einsum("pac,cd->pad", whole, pair, preferred_element_type=jnp.float32).astype(jnp.bfloat16)
    ladder = jnp.einsum("pad,pbd->ab", dressed, whole, preferred_element_type=jnp.float32)
    swapped = jnp.roll(ladder, (half, half), (0, 1))
    ladder_term = jnp.where(core == 0, ladder, swapped).astype(jnp.bfloat16).reshape(amplitudes.shape)
    parts = tied(parts, ladder_term)
    total = jnp.sum(parts.reshape(pairs, 2, 2, width, outs).astype(jnp.float32), axis=0)
    total = jnp.transpose(total, (1, 0, 2, 3)).reshape(4 * width, outs).astype(jnp.bfloat16)
    cycle_term = in_order(total[:, :part], total[:, part:], "core", 1)

    return (ladder_term, cycle_term)


def solution(mesh):
    groups, rows, cols = mesh.devices.shape
    split = Mesh(mesh.devices.reshape(groups // 2, 2, rows // 2, 2, 2, cols // 2), AXES)
    row, col = ("rowpair", "side"), ("lo", "z")
    pairs = P(("hi", "core", *row), col, None, None)
    return jax.shard_map(
        body,
        mesh=split,
        in_specs=(pairs, P(col, None, None), P(col, row), P()),
        out_specs=(pairs, P(("hi", "core", *row), col)),
        check_vma=False,
    )
```

```python
import jax
import jax.numpy as jnp
from jax import lax
from jax.experimental import pallas as pl
from jax.experimental.pallas import tpu as pltpu
from jax.sharding import Mesh, PartitionSpec as P

VMEM = 20 * 1024 * 1024
AXES = ("hi", "core", "rowpair", "side", "lo", "z")


SHIFTS = (3, -3, 2, -2, 1, -1, 4)


def shift(x, by):
    depth = lax.axis_size("z")
    return lax.ppermute(x, "z", [(i, (i + by) % depth) for i in range(depth)])


def swap(x, axis):
    return lax.ppermute(x, axis, [(0, 1), (1, 0)])


def tied(x, *after):
    return lax.optimization_barrier((x, *after))[0]


def exchange(x, axes):
    return lax.all_to_all(x, axes, 0, 0, tiled=True)


def join_kernel(*refs):
    pieces, out_ref = refs[:-1], refs[-1]
    count = pieces[0].shape[0]
    for i, piece in enumerate(pieces):
        out_ref[pl.ds(i * count, count)] = piece[...]


def joined(blocks):
    shape = (len(blocks) * blocks[0].shape[0], *blocks[0].shape[1:])
    size = 4 * blocks[0].size * len(blocks)
    return pl.pallas_call(
        join_kernel,
        in_specs=[pl.BlockSpec(memory_space=pltpu.VMEM)] * len(blocks),
        out_specs=pl.BlockSpec(memory_space=pltpu.VMEM),
        out_shape=jax.ShapeDtypeStruct(shape, blocks[0].dtype),
        cost_estimate=pl.CostEstimate(flops=0, bytes_accessed=size, transcendentals=0),
        compiler_params=pltpu.CompilerParams(vmem_limit_bytes=VMEM),
        name="join",
    )(*blocks)


def product_kernel(near_ref, far_ref, weight_ref, near_other_ref, last_other_ref, out_ref, own_ref, sems):
    core, low = lax.axis_index("core"), lax.axis_index("lo")
    count = near_ref.shape[0]
    part, inner = near_other_ref.shape
    halves = [pl.ds(pl.multiple_of(at * part, part), part) for at in (core, 1 - core)]
    copies = [pltpu.make_async_copy(weight_ref.at[rows], own_ref.at[i], sems.at[i]) for i, rows in enumerate(halves)]
    for copy in copies:
        copy.start()

    def term(weight, at):
        panel = jnp.concatenate([near_ref[:, at : at + inner], far_ref[:, at : at + inner]], axis=0)
        return lax.dot_general(weight, panel, (((1,), (1,)), ((), ())), preferred_element_type=jnp.float32)

    others = [term(ref[...], inner) for ref in (near_other_ref, last_other_ref)]
    for i, rows in enumerate(halves):
        copies[i].wait()
        sums = (term(own_ref[i], 0) + others[i]).T.astype(out_ref.dtype)
        out_ref[pl.ds(pl.multiple_of(low * count, count), count), rows] = sums[:count]
        out_ref[pl.ds(pl.multiple_of((1 - low) * count, count), count), rows] = sums[count:]


def products(near, far, *weights):
    count, outs = near.shape[0], weights[0].shape[0]
    flops = 4 * near.size * outs
    return pl.pallas_call(
        product_kernel,
        in_specs=[pl.BlockSpec(memory_space=pl.ANY if i == 2 else pltpu.VMEM) for i in range(5)],
        out_specs=pl.BlockSpec(memory_space=pltpu.VMEM),
        out_shape=jax.ShapeDtypeStruct((2 * count, outs), jnp.bfloat16),
        scratch_shapes=[pltpu.VMEM((2, outs // 2, near.shape[1] // 2), jnp.bfloat16), pltpu.SemaphoreType.DMA((2,))],
        cost_estimate=pl.CostEstimate(flops=flops, bytes_accessed=8 * outs * near.shape[1], transcendentals=0),
        compiler_params=pltpu.CompilerParams(vmem_limit_bytes=44 * 1024 * 1024),
        name="products",
    )(near, far, *weights)


def body(amplitudes, factors, cycle_weight, orbital_order):
    virtual = amplitudes.shape[2]
    pair = amplitudes.reshape(virtual, virtual)
    groups = lax.axis_size("hi") * lax.axis_size("core")
    pairs = lax.axis_size("rowpair")
    depth = lax.axis_size("z")
    occupied = groups * pairs * 2
    width = virtual // groups // 2
    block = virtual // pairs
    outs, inner = cycle_weight.shape
    core = lax.axis_index("core")

    half = virtual // 2
    mine = lax.dynamic_slice_in_dim(factors, core * half, half, axis=1)
    both = jnp.concatenate([mine, swap(mine, "lo")])

    pick = (orbital_order[:, None] == jnp.arange(virtual, dtype=jnp.int32)[None, :]).astype(jnp.bfloat16)
    ordered = jnp.einsum("xd,cd->xc", pick, pair, preferred_element_type=jnp.float32).astype(jnp.bfloat16)
    tiles = ordered.reshape(groups, 2, width, pairs, block)
    tiles = jnp.transpose(tiles, (0, 3, 1, 2, 4)).reshape(occupied, width * block // 128, 128)
    arrived = exchange(tiles, ("hi", "core", "rowpair", "side"))

    part = outs // 2
    near_weight = lax.dynamic_slice_in_dim(cycle_weight, core * part, part, axis=0)
    near_other = swap(near_weight, "side")
    last_other = swap(near_other, "core")

    own = arrived.reshape(occupied, width, 2, block // 2)
    own = jnp.transpose(own, (2, 1, 3, 0)).reshape(2, width, inner)
    first = lax.axis_index("side") == 0
    own = jnp.concatenate([jnp.where(first, own[0], own[1]), jnp.where(first, own[1], own[0])], axis=1)

    copies = jnp.broadcast_to(own, (depth, *own.shape))
    near = exchange(copies, "z")
    blocks = [both] + [shift(both, by) for by in SHIFTS]

    far = swap(near, "lo")
    near, far = near.reshape(depth * width, -1), far.reshape(depth * width, -1)
    parts = products(near, far, cycle_weight, near_other, last_other).reshape(2 * pairs, -1, outs)
    parts = exchange(parts, ("rowpair", "side"))
    halves = joined(blocks)
    others = swap(halves, "core")
    whole = jnp.concatenate([halves, others], axis=1)
    dressed = jnp.einsum("pac,cd->pad", whole, pair, preferred_element_type=jnp.float32).astype(jnp.bfloat16)
    ladder = jnp.einsum("pad,pbd->ab", dressed, whole, preferred_element_type=jnp.float32)
    swapped = jnp.roll(ladder, (half, half), (0, 1))
    ladder_term = jnp.where(core == 0, ladder, swapped).astype(jnp.bfloat16).reshape(amplitudes.shape)
    parts = tied(parts, ladder_term)
    total = jnp.sum(parts.reshape(pairs, 2, 2, width, outs).astype(jnp.float32), axis=0)
    cycle_term = jnp.transpose(total, (1, 0, 2, 3)).reshape(4 * width, outs).astype(jnp.bfloat16)

    return (ladder_term, cycle_term)


def solution(mesh):
    groups, rows, cols = mesh.devices.shape
    split = Mesh(mesh.devices.reshape(groups // 2, 2, rows // 2, 2, 2, cols // 2), AXES)
    row, col = ("rowpair", "side"), ("lo", "z")
    pairs = P(("hi", "core", *row), col, None, None)
    return jax.shard_map(
        body,
        mesh=split,
        in_specs=(pairs, P(col, None, None), P(col, row), P()),
        out_specs=(pairs, P(("hi", "core", *row), col)),
        check_vma=False,
    )
```

```python
import jax
import jax.numpy as jnp
from jax import lax
from jax.experimental import pallas as pl
from jax.experimental.pallas import tpu as pltpu
from jax.sharding import Mesh, PartitionSpec as P

VMEM = 20 * 1024 * 1024
PRODUCT_VMEM = 52 * 1024 * 1024
AXES = ("hi", "core", "row", "lo", "z")


def shift(x, by):
    depth = lax.axis_size("z")
    return lax.ppermute(x, "z", [(i, (i + by) % depth) for i in range(depth)])


def swap(x, axis):
    return lax.ppermute(x, axis, [(0, 1), (1, 0)])


def exchange(x, axes):
    return lax.all_to_all(x, axes, 0, 0, tiled=True)


def join_kernel(*refs):
    pieces, out_ref = refs[:-1], refs[-1]
    at = 0
    for piece in pieces:
        out_ref[pl.ds(at, piece.shape[0])] = piece[...]
        at += piece.shape[0]


def joined(blocks):
    shape = (sum(b.shape[0] for b in blocks), *blocks[0].shape[1:])
    size = 4 * sum(b.size for b in blocks)
    return pl.pallas_call(
        join_kernel,
        in_specs=[pl.BlockSpec(memory_space=pltpu.VMEM)] * len(blocks),
        out_specs=pl.BlockSpec(memory_space=pltpu.VMEM),
        out_shape=jax.ShapeDtypeStruct(shape, blocks[0].dtype),
        cost_estimate=pl.CostEstimate(flops=0, bytes_accessed=size, transcendentals=0),
        compiler_params=pltpu.CompilerParams(vmem_limit_bytes=VMEM),
        name="join",
    )(*blocks)


def product_kernel(near_ref, far_ref, weight_ref, out_ref, held, sems):
    low = lax.axis_index("lo")
    count = near_ref.shape[0]
    steps, tile, _ = held.shape
    copies = [pltpu.make_async_copy(weight_ref.at[pl.ds(i * tile, tile)], held.at[i], sems.at[i]) for i in range(steps)]
    for copy in copies:
        copy.start()
    panel = jnp.concatenate([near_ref[...], far_ref[...]], axis=0)
    for i in range(steps):
        copies[i].wait()
        sums = lax.dot_general(held[i], panel, (((1,), (1,)), ((), ())), preferred_element_type=jnp.float32)
        sums = sums.T.astype(out_ref.dtype)
        columns = pl.ds(i * tile, tile)
        out_ref[pl.ds(pl.multiple_of(low * count, count), count), columns] = sums[:count]
        out_ref[pl.ds(pl.multiple_of((1 - low) * count, count), count), columns] = sums[count:]


def products(near, far, weight):
    count, outs = near.shape[0], weight.shape[0]
    steps = 4
    return pl.pallas_call(
        product_kernel,
        in_specs=[pl.BlockSpec(memory_space=pl.ANY if i == 2 else pltpu.VMEM) for i in range(3)],
        out_specs=pl.BlockSpec(memory_space=pltpu.VMEM),
        out_shape=jax.ShapeDtypeStruct((2 * count, outs), jnp.bfloat16),
        scratch_shapes=[
            pltpu.VMEM((steps, outs // steps, weight.shape[1]), jnp.bfloat16),
            pltpu.SemaphoreType.DMA((steps,)),
        ],
        cost_estimate=pl.CostEstimate(
            flops=4 * near.size * outs, bytes_accessed=2 * weight.size + 8 * near.size, transcendentals=0
        ),
        compiler_params=pltpu.CompilerParams(vmem_limit_bytes=PRODUCT_VMEM),
        name="products",
    )(near, far, weight)


def body(amplitudes, factors, cycle_weight, orbital_order):
    virtual = amplitudes.shape[2]
    pair = amplitudes.reshape(virtual, virtual)
    groups = lax.axis_size("hi") * lax.axis_size("core")
    rows = lax.axis_size("row")
    depth = lax.axis_size("z")
    width = virtual // groups
    block = virtual // rows
    outs, inner = cycle_weight.shape
    core = lax.axis_index("core")

    half = virtual // 2
    mine = lax.dynamic_slice_in_dim(factors, core * half, half, axis=1)
    both = jnp.concatenate([mine, swap(mine, "lo")])

    pick = (orbital_order[:, None] == jnp.arange(virtual, dtype=jnp.int32)[None, :]).astype(jnp.bfloat16)
    ordered = jnp.einsum("xd,cd->xc", pick, pair, preferred_element_type=jnp.float32).astype(jnp.bfloat16)
    tiles = ordered.reshape(groups, width, rows, block)
    tiles = jnp.transpose(tiles, (0, 2, 1, 3)).reshape(groups * rows, width * block // 128, 128)
    arrived = exchange(tiles, ("hi", "core", "row"))
    own = arrived.reshape(groups * rows, width, block)
    own = jnp.transpose(own, (1, 2, 0)).reshape(width, inner)

    chunk = width // 2

    def gathered(part):
        copies = jnp.broadcast_to(part, (depth, *part.shape))
        return exchange(copies, "z").reshape(depth * chunk, inner)

    near_a = gathered(own[:chunk])
    near_b = gathered(own[chunk:])
    far_a = swap(near_a, "lo")
    far_b = swap(near_b, "lo")

    left = shift(both, 1)
    right = shift(both, -1)
    left_two = shift(jnp.concatenate([both, left]), 2)
    right_two = shift(jnp.concatenate([both, right]), -2)
    opposite = shift(both, depth // 2)

    def summed(near, far):
        parts = products(near, far, cycle_weight).reshape(rows, -1, outs)
        parts = exchange(parts, "row")
        total = jnp.sum(parts.astype(jnp.float32), axis=0).astype(jnp.bfloat16)
        return total.reshape(-1, chunk, outs)

    total_a = summed(near_a, far_a)
    total_b = summed(near_b, far_b)
    cycle_term = jnp.concatenate([total_a, total_b], axis=1).reshape(-1, outs)

    halves = joined([both, left, right, left_two, right_two, opposite])
    others = swap(halves, "core")
    whole = jnp.concatenate([halves, others], axis=1)
    dressed = jnp.einsum("pac,cd->pad", whole, pair, preferred_element_type=jnp.float32).astype(jnp.bfloat16)
    ladder = jnp.einsum("pad,pbd->ab", dressed, whole, preferred_element_type=jnp.float32)
    swapped = jnp.roll(ladder, (half, half), (0, 1))
    ladder_term = jnp.where(core == 0, ladder, swapped).astype(jnp.bfloat16).reshape(amplitudes.shape)
    return (ladder_term, cycle_term)


def solution(mesh):
    groups, rows, cols = mesh.devices.shape
    split = Mesh(mesh.devices.reshape(groups // 2, 2, rows, 2, cols // 2), AXES)
    row, col = "row", ("lo", "z")
    pairs = P(("hi", "core", row), col, None, None)
    return jax.shard_map(
        body,
        mesh=split,
        in_specs=(pairs, P(col, None, None), P(col, row), P()),
        out_specs=(pairs, P(("hi", "core", row), col)),
        check_vma=False,
    )
```

```python
import jax
import jax.numpy as jnp
from jax import lax
from jax.experimental import pallas as pl
from jax.experimental.pallas import tpu as pltpu
from jax.sharding import Mesh, PartitionSpec as P

VMEM = 20 * 1024 * 1024
HALF_VMEM = 50 * 1024 * 1024
AXES = ("hi", "core", "rowpair", "side", "lo", "z")


SHIFTS = (3, -3, 2, -2, 4, 1, -1)


def shift(x, by):
    depth = lax.axis_size("z")
    return lax.ppermute(x, "z", [(i, (i + by) % depth) for i in range(depth)])


def swap(x, axis):
    return lax.ppermute(x, axis, [(0, 1), (1, 0)])


def tied(x, *after):
    return lax.optimization_barrier((x, *after))[0]


def exchange(x, axes):
    return lax.all_to_all(x, axes, 0, 0, tiled=True)


def join_kernel(*refs):
    pieces, out_ref = refs[:-1], refs[-1]
    count = pieces[0].shape[0]
    for i, piece in enumerate(pieces):
        out_ref[pl.ds(i * count, count)] = piece[...]


def joined(blocks):
    shape = (len(blocks) * blocks[0].shape[0], *blocks[0].shape[1:])
    size = 4 * blocks[0].size * len(blocks)
    return pl.pallas_call(
        join_kernel,
        in_specs=[pl.BlockSpec(memory_space=pltpu.VMEM)] * len(blocks),
        out_specs=pl.BlockSpec(memory_space=pltpu.VMEM),
        out_shape=jax.ShapeDtypeStruct(shape, blocks[0].dtype),
        cost_estimate=pl.CostEstimate(flops=0, bytes_accessed=size, transcendentals=0),
        compiler_params=pltpu.CompilerParams(vmem_limit_bytes=VMEM),
        name="join",
    )(*blocks)


def half_kernel(weight_ref, out_ref, sem):
    part = out_ref.shape[0]
    rows = pl.ds(pl.multiple_of(lax.axis_index("core") * part, part), part)
    copy = pltpu.make_async_copy(weight_ref.at[rows], out_ref, sem)
    copy.start()
    copy.wait()


def half_of(weight, part):
    shape = (part, weight.shape[1])
    return pl.pallas_call(
        half_kernel,
        in_specs=[pl.BlockSpec(memory_space=pl.ANY)],
        out_specs=pl.BlockSpec(memory_space=pltpu.VMEM),
        out_shape=jax.ShapeDtypeStruct(shape, weight.dtype),
        scratch_shapes=[pltpu.SemaphoreType.DMA],
        cost_estimate=pl.CostEstimate(flops=0, bytes_accessed=2 * weight.size, transcendentals=0),
        compiler_params=pltpu.CompilerParams(vmem_limit_bytes=HALF_VMEM),
        name="half",
    )(weight)


def product_kernel(near_ref, far_ref, weight_ref, near_other_ref, last_other_ref, out_ref, own_ref, sems):
    core, low = lax.axis_index("core"), lax.axis_index("lo")
    count = near_ref.shape[0]
    part, inner = near_other_ref.shape
    halves = [pl.ds(pl.multiple_of(at * part, part), part) for at in (core, 1 - core)]
    sources = [weight_ref.at[rows] for rows in halves] + [near_other_ref]
    copies = [pltpu.make_async_copy(source, own_ref.at[i], sems.at[i]) for i, source in enumerate(sources)]
    for copy in reversed(copies):
        copy.start()

    def term(weight, at):
        panel = jnp.concatenate([near_ref[:, at : at + inner], far_ref[:, at : at + inner]], axis=0)
        return lax.dot_general(weight, panel, (((1,), (1,)), ((), ())), preferred_element_type=jnp.float32)

    last = term(last_other_ref[...], inner)
    copies[2].wait()
    others = [term(own_ref[2], inner), last]
    for i, rows in enumerate(halves):
        copies[i].wait()
        sums = (term(own_ref[i], 0) + others[i]).T.astype(out_ref.dtype)
        out_ref[pl.ds(pl.multiple_of(low * count, count), count), rows] = sums[:count]
        out_ref[pl.ds(pl.multiple_of((1 - low) * count, count), count), rows] = sums[count:]


def products(near, far, *weights):
    count, outs = near.shape[0], weights[0].shape[0]
    flops = 4 * near.size * outs
    return pl.pallas_call(
        product_kernel,
        in_specs=[pl.BlockSpec(memory_space=pl.ANY if i in (2, 3) else pltpu.VMEM) for i in range(5)],
        out_specs=pl.BlockSpec(memory_space=pltpu.VMEM),
        out_shape=jax.ShapeDtypeStruct((2 * count, outs), jnp.bfloat16),
        scratch_shapes=[pltpu.VMEM((3, outs // 2, near.shape[1] // 2), jnp.bfloat16), pltpu.SemaphoreType.DMA((3,))],
        cost_estimate=pl.CostEstimate(flops=flops, bytes_accessed=8 * outs * near.shape[1], transcendentals=0),
        compiler_params=pltpu.CompilerParams(vmem_limit_bytes=44 * 1024 * 1024),
        name="products",
    )(near, far, *weights)


def body(amplitudes, factors, cycle_weight, orbital_order):
    virtual = amplitudes.shape[2]
    pair = amplitudes.reshape(virtual, virtual)
    groups = lax.axis_size("hi") * lax.axis_size("core")
    pairs = lax.axis_size("rowpair")
    depth = lax.axis_size("z")
    occupied = groups * pairs * 2
    width = virtual // groups // 2
    block = virtual // pairs
    outs, inner = cycle_weight.shape
    core = lax.axis_index("core")

    half = virtual // 2
    mine = lax.dynamic_slice_in_dim(factors, core * half, half, axis=1)
    both = jnp.concatenate([mine, swap(mine, "lo")])

    pick = (orbital_order[:, None] == jnp.arange(virtual, dtype=jnp.int32)[None, :]).astype(jnp.bfloat16)
    ordered = jnp.einsum("xd,cd->xc", pick, pair, preferred_element_type=jnp.float32).astype(jnp.bfloat16)
    tiles = ordered.reshape(groups, 2, width, pairs, block)
    tiles = jnp.transpose(tiles, (0, 3, 1, 2, 4)).reshape(occupied, width * block // 128, 128)
    arrived = exchange(tiles, ("hi", "core", "rowpair", "side"))

    part = outs // 2
    near_weight = half_of(cycle_weight, part)
    near_other = swap(near_weight, "side")
    last_other = swap(near_other, "core")

    own = arrived.reshape(occupied, width, 2, block // 2)
    own = jnp.transpose(own, (2, 1, 3, 0)).reshape(2, width, inner)
    first = lax.axis_index("side") == 0
    own = jnp.concatenate([jnp.where(first, own[0], own[1]), jnp.where(first, own[1], own[0])], axis=1)

    copies = jnp.broadcast_to(own, (depth, *own.shape))
    near = exchange(copies, "z")
    blocks = [both] + [shift(both, by) for by in SHIFTS]

    far = swap(near, "lo")
    near, far = near.reshape(depth * width, -1), far.reshape(depth * width, -1)
    parts = products(near, far, cycle_weight, near_other, last_other).reshape(2 * pairs, -1, outs)
    parts = exchange(parts, ("rowpair", "side"))
    halves = joined(blocks)
    others = swap(halves, "core")
    whole = jnp.concatenate([halves, others], axis=1)
    dressed = jnp.einsum("pac,cd->pad", whole, pair, preferred_element_type=jnp.float32).astype(jnp.bfloat16)
    ladder = jnp.einsum("pad,pbd->ab", dressed, whole, preferred_element_type=jnp.float32)
    swapped = jnp.roll(ladder, (half, half), (0, 1))
    ladder_term = jnp.where(core == 0, ladder, swapped).astype(jnp.bfloat16).reshape(amplitudes.shape)
    parts = tied(parts, ladder_term)
    total = jnp.sum(parts.reshape(pairs, 2, 2, width, outs).astype(jnp.float32), axis=0)
    cycle_term = jnp.transpose(total, (1, 0, 2, 3)).reshape(4 * width, outs).astype(jnp.bfloat16)

    return (ladder_term, cycle_term)


def solution(mesh):
    groups, rows, cols = mesh.devices.shape
    split = Mesh(mesh.devices.reshape(groups // 2, 2, rows // 2, 2, 2, cols // 2), AXES)
    row, col = ("rowpair", "side"), ("lo", "z")
    pairs = P(("hi", "core", *row), col, None, None)
    return jax.shard_map(
        body,
        mesh=split,
        in_specs=(pairs, P(col, None, None), P(col, row), P()),
        out_specs=(pairs, P(("hi", "core", *row), col)),
        check_vma=False,
    )
```
